512 devices in a mesh: segment: 8 (over x, core), dp: 64 (over z, y).
Axes of the slice: x: 4, y: 8, z: 8, core: 2. Of those that a mesh axis runs over, the one named last changes fastest.
Arguments:
- latents: bfloat16 [2, 8192, 3072], P(None, 'dp'), may hold values from -70 to 70
- proj: bfloat16 [8, 3072, 1536], P('segment', 'dp'), may hold values from -0.109375 to 0.109375
- temper: float32 [8, 12], P('segment'), may hold values from 0.3 to 24
- blocks: int32 [2, 128, 12, 2], P(None, 'dp'), may hold values from 0 to 5
Outputs:
- states: bfloat16 [8, 2, 8192, 3072], P('segment', None, 'dp')
The draws below stay inside these ranges and needn't reach their ends.
All inputs are finite; a program needn't handle non-finite values.
Results may differ from the reference program's by a relative error of at most 0.013.
Values may be sent and summed in bfloat16 or wider, within the bound.
No kernel may reach another device: no remote copies, remote signals or barrier semaphores. Data moves between devices by JAX's collectives and lax.ppermute only.
A program may use at most 64 MiB of HBM per device.

```python
import math
import jax
import jax.numpy as jnp
from jax import lax

D = 3072
HEADS = 12
HD = 128
BLOCK = 64
SEL = 2
MICRO = 2
TOK_DEV = 128
WID = 1536
LAYERS = 8
TOKENS = 8192
SEQ = 4096
BPD = 2


def draw_latents(key, part):
    key_base = jax.random.fold_in(key, 0)
    base = jnp.clip(jax.random.normal(key_base, (MICRO, TOKENS, D), jnp.float32), -6.0, 6.0)
    result = base
    return result.astype(jnp.bfloat16)


def draw_temper(key, part):
    unit = jax.random.uniform(key, (LAYERS, HEADS), jnp.float32)
    upper = 2.0
    lower = 0.3
    return jnp.exp(jnp.log(lower) + unit * (jnp.log(upper) - jnp.log(lower)))


def place_ends(drawn, stream_key, low, top_value):
    longest = drawn.shape.index(max(drawn.shape))
    spots = []
    for shift in (0, 1):
        where = [jax.random.randint(jax.random.fold_in(stream_key, axis), (), 0, length) for axis, length in enumerate(drawn.shape)]
        where[longest] = (where[longest] + shift) % drawn.shape[longest]
        spots.append(tuple(where))
    return drawn.at[spots[0]].set(low).at[spots[1]].set(top_value)


def steps_of(stream_key, shape, shards, low, largest):
    def one(axis_at, blocks):
        steps = jax.random.uniform(jax.random.fold_in(jax.random.fold_in(stream_key, 6), axis_at), (blocks,), jnp.float32, low / len(shards), largest / len(shards))
        return jnp.repeat(jnp.exp(steps), shape[axis_at] // blocks).reshape((-1,) + (1,) * (len(shape) - axis_at - 1))

    level = one(*shards[0])
    for cut in shards[1:]:
        level = level * one(*cut)
    return level


def bell_draw(key, dims, width, bound, cuts=(), held_as=jnp.bfloat16):
    loudness = steps_of(key, dims, cuts, -0.22, 0.18) if cuts else 1.0
    array = jax.random.normal(key, dims, jnp.float32) * width * loudness
    return jnp.minimum(jnp.maximum(array, -bound), bound).astype(held_as)


def setup_inputs(seed: int = 0) -> dict:
    key_list = jax.random.split(jax.random.key(seed), 5)
    return {
        "latents": draw_latents(jax.random.fold_in(key_list[4], 71), 0),
        "proj": bell_draw(key_list[1], (LAYERS, D, WID), D ** -0.5, 0.109375, ((0, 8), (1, 64))),
        "temper": draw_temper(jax.random.fold_in(key_list[4], 71), 0),
        "blocks": place_ends(jax.random.randint(key_list[3], (MICRO, TOKENS // BLOCK, HEADS, SEL), 0, 3 * BPD), jax.random.fold_in(key_list[3], 1), 0, (3 * BPD) - 1).astype(jnp.int32),
    }


epsilon = 1e-06

def unit_heads(values, head_count):
    shaped = values.astype(jnp.float32).reshape(values.shape[:-1] + (head_count, -1))
    return (shaped * lax.rsqrt(lax.optimization_barrier(jnp.mean(shaped * shaped, axis=-1, keepdims=True)) + epsilon)).astype(jnp.bfloat16)

def layer(hidden, weight, temp, chosen):
    h_float = hidden.astype(jnp.float32)
    normed = (h_float * lax.rsqrt(lax.optimization_barrier(jnp.mean(h_float * h_float, axis=-1, keepdims=True)) + epsilon)).astype(jnp.bfloat16)
    values = jnp.dot(normed, weight, preferred_element_type=jnp.float32).astype(jnp.bfloat16)
    total_blocks = TOKENS // BLOCK
    per_dev = TOK_DEV // BLOCK
    seq_blocks = SEQ // BLOCK
    keys = unit_heads(values, HEADS).reshape(total_blocks, BLOCK, HEADS, HD)
    vals = values.reshape(total_blocks, BLOCK, HEADS, HD)
    query_block = jnp.arange(total_blocks, dtype=jnp.int32)
    absolute = ((query_block // per_dev - 1) * per_dev)[:, None, None] + chosen
    usable = (absolute >= 0) & (absolute < total_blocks) & (absolute // seq_blocks == (query_block // seq_blocks)[:, None, None])
    clipped = jnp.clip(absolute, 0, total_blocks - 1).astype(jnp.int32)
    head_index = jnp.arange(HEADS, dtype=jnp.int32)[None, :, None]
    keys_by_head = jnp.transpose(keys, (2, 0, 1, 3))
    vals_by_head = jnp.transpose(vals, (2, 0, 1, 3))
    key_pick = keys_by_head[head_index, clipped]
    val_pick = vals_by_head[head_index, clipped]
    score_scale = temp * (1.0 / math.sqrt(HD))
    keys_float = keys.astype(jnp.float32)
    own = jnp.einsum('bihd,bjhd->bhij', keys_float, keys_float) * score_scale[None, :, None, None]
    diag = jnp.eye(BLOCK, dtype=bool)
    own = jnp.where(diag[None, None], -jnp.inf, own)
    picked = jnp.einsum('bihd,bhsjd->bhisj', keys_float, key_pick.astype(jnp.float32)) * score_scale[None, :, None, None, None]
    same_block = absolute == query_block[:, None, None]
    keep = usable[:, :, None, :, None] & ~(same_block[:, :, None, :, None] & diag[None, None, :, None, :])
    picked = jnp.where(keep, picked, -jnp.inf)
    joined = jnp.concatenate([own, picked.reshape(total_blocks, HEADS, BLOCK, SEL * BLOCK)], axis=-1)
    weights = jax.nn.softmax(joined, axis=-1).astype(jnp.bfloat16)
    w_own = weights[..., :BLOCK].astype(jnp.float32)
    w_pick = weights[..., BLOCK:].reshape(total_blocks, HEADS, BLOCK, SEL, BLOCK).astype(jnp.float32)
    mixed = jnp.einsum('bhij,bjhd->bihd', w_own, vals.astype(jnp.float32))
    mixed = mixed + jnp.einsum('bhisj,bhsjd->bihd', w_pick, val_pick.astype(jnp.float32))
    mixed = mixed.reshape(TOKENS, WID).astype(jnp.bfloat16)
    return (h_float + jnp.dot(mixed, weight.T, preferred_element_type=jnp.float32)).astype(jnp.bfloat16)

def reference(latents, proj, temper, blocks):
    per_micro = []
    for slot in range(MICRO):
        hidden = latents[slot]
        layer_rows = []
        for depth in range(LAYERS):
            hidden = layer(hidden, proj[depth], temper[depth], blocks[slot])
            layer_rows.append(hidden)
        per_micro.append(jnp.stack(layer_rows))
    return jnp.stack(per_micro, axis=1)
```

```python
import functools
import math

import jax
import jax.numpy as jnp
from jax import lax
from jax.experimental import pallas as pl
from jax.experimental.pallas import tpu as pltpu
from jax.sharding import Mesh, PartitionSpec as P

BLOCK = 64
EPS = 1e-06
NEG = -1e30
NT = (((1,), (1,)), ((), ()))


def weight_copies(source, buffer, sems, first_row, by_rows, chunk):
    rows, cols = buffer.shape
    copies = []
    for i in range((rows if by_rows else cols) // chunk):
        if by_rows:
            src = source.at[pl.ds(first_row + i * chunk, chunk), :]
            dst = buffer.at[pl.ds(i * chunk, chunk), :]
        else:
            src = source.at[pl.ds(first_row, rows), pl.ds(i * chunk, chunk)]
            dst = buffer.at[:, pl.ds(i * chunk, chunk)]
        copies.append(pltpu.make_async_copy(src, dst, sems.at[i]))
    return copies


def attend_heads(scale_ref, bias_ref, before_ref, own_ref, after_ref, mixed_ref, layer):
    tok, feat = own_ref.shape
    heads = feat // 128
    row = lax.broadcasted_iota(jnp.int32, (tok, tok), 0)
    col = lax.broadcasted_iota(jnp.int32, (tok, tok), 1)
    diag = row == col

    def unit(values):
        wide = values.astype(jnp.float32)
        mean = jnp.mean(wide * wide, axis=-1, keepdims=True)
        return (wide * lax.rsqrt(mean + EPS)).astype(jnp.bfloat16)

    for h in range(heads):
        at = pl.ds(h * 128, 128)
        parts = [before_ref[:, at], own_ref[:, at], after_ref[:, at]]
        keys = [unit(p) for p in parts]
        factor = scale_ref[layer, h]
        scores = []
        for i, k in enumerate(keys):
            s = lax.dot_general(keys[1], k, NT, preferred_element_type=jnp.float32) * factor
            upper = bias_ref[2 * h : 2 * h + 1, i * tok : (i + 1) * tok]
            lower = bias_ref[2 * h + 1 : 2 * h + 2, i * tok : (i + 1) * tok]
            bias = jnp.concatenate(
                [
                    jnp.broadcast_to(upper, (tok // 2, tok)),
                    jnp.broadcast_to(lower, (tok // 2, tok)),
                ],
                axis=0,
            )
            s = s + bias
            if i == 1:
                s = jnp.where(diag, NEG, s)
            scores.append(s)
        top = jnp.max(
            jnp.maximum(jnp.maximum(scores[0], scores[1]), scores[2]), axis=-1, keepdims=True
        )
        probs = [jnp.exp2(s - top) for s in scores]
        total = jnp.sum(probs[0] + probs[1] + probs[2], axis=-1, keepdims=True)
        acc = jnp.zeros((tok, 128), jnp.float32)
        for p, v in zip(probs, parts):
            acc = acc + jnp.dot(p.astype(jnp.bfloat16), v, preferred_element_type=jnp.float32)
        mixed_ref[:, at] = (acc / total).astype(jnp.bfloat16)


def project_chunks(hidden_ref, values_ref, normed_ref, buffer, copies, chunk):
    wide = hidden_ref[...].astype(jnp.float32)
    mean = jnp.mean(wide * wide, axis=-1, keepdims=True)
    normed_ref[...] = (wide * lax.rsqrt(mean + EPS)).astype(jnp.bfloat16)
    for i, copy in enumerate(copies):
        copy.wait()
        at = pl.ds(i * chunk, chunk)
        values_ref[:, at] = jnp.dot(
            normed_ref[...], buffer[:, at], preferred_element_type=jnp.float32
        ).astype(jnp.bfloat16)


def finish_chunks(hidden_ref, mixed_ref, out_ref, buffer, copies, chunk):
    for i, copy in enumerate(copies):
        copy.wait()
        at = pl.ds(i * chunk, chunk)
        back = lax.dot_general(
            mixed_ref[...], buffer[at, :], NT, preferred_element_type=jnp.float32
        )
        out_ref[:, at] = (hidden_ref[:, at].astype(jnp.float32) + back).astype(jnp.bfloat16)


def enter_kernel(chunk, first, hidden_ref, weight_ref, values_ref, buffer, normed_ref, sems):
    copies = weight_copies(weight_ref, buffer, sems, first, False, chunk)
    for copy in copies:
        copy.start()
    project_chunks(hidden_ref, values_ref, normed_ref, buffer, copies, chunk)


def inner_kernel(
    chunk, layer, first, second,
    scale_ref, bias_ref, before_ref, own_ref, after_ref, hidden_ref, weight_ref,
    out_ref, values_ref,
    buffer, later, mixed_ref, normed_ref, sems, later_sems,
):
    copies = weight_copies(weight_ref, buffer, sems, first, True, chunk)
    nexts = weight_copies(weight_ref, later, later_sems, second, False, chunk)
    for copy in copies + nexts:
        copy.start()
    attend_heads(scale_ref, bias_ref, before_ref, own_ref, after_ref, mixed_ref, layer)
    finish_chunks(hidden_ref, mixed_ref, out_ref, buffer, copies, chunk)
    project_chunks(out_ref, values_ref, normed_ref, later, nexts, chunk)


def leave_kernel(
    chunk, layer, first,
    scale_ref, bias_ref, before_ref, own_ref, after_ref, hidden_ref, weight_ref,
    out_ref,
    buffer, mixed_ref, sems,
):
    copies = weight_copies(weight_ref, buffer, sems, first, True, chunk)
    for copy in copies:
        copy.start()
    attend_heads(scale_ref, bias_ref, before_ref, own_ref, after_ref, mixed_ref, layer)
    finish_chunks(hidden_ref, mixed_ref, out_ref, buffer, copies, chunk)


VM = pl.BlockSpec(memory_space=pltpu.VMEM)
SM = pl.BlockSpec(memory_space=pltpu.SMEM)
ANY = pl.BlockSpec(memory_space=pl.ANY)
CHUNK = 512


def params():
    return pltpu.CompilerParams(vmem_limit_bytes=48 << 20)


def cost(flops, moved):
    return pl.CostEstimate(flops=int(flops), bytes_accessed=int(moved), transcendentals=0)


def kernels(tok, width, feat):
    bf = jnp.bfloat16
    weight = pltpu.VMEM((width, feat), bf)
    mixed = pltpu.VMEM((tok, feat), bf)
    normed = pltpu.VMEM((tok, width), bf)
    by_col = pltpu.SemaphoreType.DMA((feat // CHUNK,))
    by_row = pltpu.SemaphoreType.DMA((width // CHUNK,))
    hidden_out = jax.ShapeDtypeStruct((tok, width), bf)
    values_out = jax.ShapeDtypeStruct((tok, feat), bf)
    product = 2 * tok * width * feat
    size = 2 * width * feat
    enter = pl.pallas_call(
        functools.partial(enter_kernel, CHUNK, 0),
        out_shape=values_out,
        in_specs=[VM, ANY],
        out_specs=VM,
        scratch_shapes=[weight, normed, by_col],
        compiler_params=params(),
        cost_estimate=cost(product, size),
    )
    inner = pl.pallas_call(
        functools.partial(inner_kernel, CHUNK, 0, 0, width),
        out_shape=(hidden_out, values_out),
        in_specs=[SM, VM, VM, VM, VM, VM, ANY],
        out_specs=(VM, VM),
        scratch_shapes=[weight, weight, mixed, normed, by_row, by_col],
        compiler_params=params(),
        cost_estimate=cost(2 * product, 2 * size),
    )
    leave = pl.pallas_call(
        functools.partial(leave_kernel, CHUNK, 1, width),
        out_shape=hidden_out,
        in_specs=[SM, VM, VM, VM, VM, VM, ANY],
        out_specs=VM,
        scratch_shapes=[weight, mixed, by_row],
        compiler_params=params(),
        cost_estimate=cost(product, size),
    )
    return enter, inner, leave


def on_device(latents, proj, temper, blocks):
    planes = lax.axis_size("x")
    plane = lax.axis_index("x")
    core = lax.axis_index("c")
    dp_count = lax.axis_size("dp")
    dp_index = lax.axis_index("dp")
    micro_count, tok, width = latents.shape
    heads = temper.shape[1]
    feat = proj.shape[2]
    per_dev = tok // BLOCK
    window = 3 * per_dev
    total_blocks = tok * dp_count // BLOCK
    seq_blocks = min(4096, tok * dp_count) // BLOCK

    weights = lax.all_gather(proj[0], ("c", "dp"), axis=0, tiled=True)
    swap = [(0, 1), (1, 0)]
    mine = temper[0]
    other = lax.ppermute(mine, "c", swap)
    both = jnp.where(core == 0, jnp.stack([mine, other]), jnp.stack([other, mine]))
    scale = both * (math.log2(math.e) / math.sqrt(feat // heads))

    chosen = lax.dynamic_index_in_dim(blocks, core, 0, keepdims=False)
    spots = jnp.arange(window, dtype=jnp.int32)
    absolute = (dp_index - 1) * per_dev + spots
    query = dp_index * per_dev + jnp.arange(per_dev, dtype=jnp.int32)
    usable = (
        (absolute >= 0)
        & (absolute < total_blocks)
        & (absolute[None, :] // seq_blocks == query[:, None] // seq_blocks)
    )
    listed = jnp.sum((chosen[..., None] == spots).astype(jnp.int32), axis=2)
    own = (spots[None, :] == per_dev + jnp.arange(per_dev)[:, None]).astype(jnp.int32)
    count = jnp.where(usable[:, None, :], listed, 0) + own[:, None, :]
    bias = jnp.where(count > 0, jnp.log2(jnp.maximum(count, 1).astype(jnp.float32)), NEG)
    bias = jnp.repeat(jnp.transpose(bias, (1, 0, 2)).reshape(heads * per_dev, window), BLOCK, axis=1)

    enter, inner, leave = kernels(tok, width, feat)
    up = [(i, i + 1) for i in range(dp_count - 1)]
    down = [(i + 1, i) for i in range(dp_count - 1)]
    hop = [(i, i + 1) for i in range(planes - 1)]

    def beside(values):
        return lax.ppermute(values, "dp", up), lax.ppermute(values, "dp", down)

    hidden = lax.dynamic_index_in_dim(latents, core, 0, keepdims=False)
    first = second = None
    for stage in range(planes):
        values = enter(hidden, weights)
        before, after = beside(values)
        middle, values = inner(scale, bias, before, values, after, hidden, weights)
        before, after = beside(values)
        final = leave(scale, bias, before, values, after, middle, weights)
        if stage < planes - 1:
            hidden = lax.ppermute(final, "x", hop)
        if stage == 0:
            first, second = middle, final
        else:
            first = jnp.where(plane == stage, middle, first)
            second = jnp.where(plane == stage, final, second)
    got = lax.ppermute(jnp.where(core == 0, second, first), "c", swap)
    states = jnp.where(core == 0, jnp.stack([first, got]), jnp.stack([got, second]))
    return states[None]


def solution(mesh):
    planes = mesh.devices.shape[0] // 2
    split = Mesh(mesh.devices.reshape(planes, 2, -1), ("x", "c", "dp"))
    placed = (
        P(None, "dp", None),
        P(("x", "c"), "dp", None),
        P(("x", "c"), None),
        P(None, "dp", None, None),
    )
    return jax.shard_map(
        on_device,
        mesh=split,
        in_specs=placed,
        out_specs=P(("x", "c"), None, "dp", None),
        check_vma=False,
    )
```

```python
import functools
import math

import jax
import jax.numpy as jnp
from jax import lax
from jax.experimental import pallas as pl
from jax.experimental.pallas import tpu as pltpu
from jax.sharding import Mesh, PartitionSpec as P

BLOCK = 64
EPS = 1e-06
NEG = -1e30
NT = (((1,), (1,)), ((), ()))


def unit(values):
    wide = values.astype(jnp.float32)
    mean = jnp.mean(wide * wide, axis=-1, keepdims=True)
    return (wide * lax.rsqrt(mean + EPS)).astype(jnp.bfloat16)


def attend_heads(layer, scale_ref, bias_ref, before_ref, own_ref, after_ref, mixed_ref):
    tok, feat = own_ref.shape
    size = 128
    half = tok // 2
    row = lax.broadcasted_iota(jnp.int32, (tok, tok), 0)
    col = lax.broadcasted_iota(jnp.int32, (tok, tok), 1)
    diag = row == col

    def window_of(h):
        at = pl.ds(h * size, size)
        return [ref[:, at] for ref in (before_ref, own_ref, after_ref)]

    def logits_of(h, keys):
        factor = scale_ref[layer, h]
        scores = lax.dot_general(
            keys[1], jnp.concatenate(keys, axis=0), NT, preferred_element_type=jnp.float32
        )
        logits = []
        for i in range(3):
            part = scores[:, i * tok : (i + 1) * tok]
            upper = bias_ref[2 * h : 2 * h + 1, i * tok : (i + 1) * tok]
            lower = bias_ref[2 * h + 1 : 2 * h + 2, i * tok : (i + 1) * tok]
            part = jnp.concatenate(
                [part[:half] * factor + upper, part[half:] * factor + lower], axis=0
            )
            logits.append(jnp.where(diag, NEG, part) if i == 1 else part)
        return logits

    def probs_of(logits):
        top = jnp.max(
            jnp.maximum(jnp.maximum(logits[0], logits[1]), logits[2]), axis=-1, keepdims=True
        )
        return [jnp.exp2(part - top) for part in logits]

    for first in range(0, feat // size, GROUP):
        heads = range(first, first + GROUP)
        windows = [window_of(h) for h in heads]
        keys = [[unit(part) for part in window] for window in windows]
        logits = [logits_of(h, k) for h, k in zip(heads, keys)]
        probs = [probs_of(part) for part in logits]
        for h, window, prob in zip(heads, windows, probs):
            acc = jnp.dot(
                jnp.concatenate([p.astype(jnp.bfloat16) for p in prob], axis=1),
                jnp.concatenate(window, axis=0),
                preferred_element_type=jnp.float32,
            )
            total = jnp.sum(prob[0] + prob[1] + prob[2], axis=-1, keepdims=True)
            mixed_ref[:, pl.ds(h * size, size)] = (acc / total).astype(jnp.bfloat16)


def project(hidden_ref, values_ref, normed_ref, weight_ref):
    normed_ref[...] = unit(hidden_ref[...])
    for i in range(weight_ref.shape[1] // CHUNK):
        at = pl.ds(i * CHUNK, CHUNK)
        values_ref[:, at] = jnp.dot(
            normed_ref[...], weight_ref[:, at], preferred_element_type=jnp.float32
        ).astype(jnp.bfloat16)


def finish(hidden_ref, mixed_ref, out_ref, turned_ref):
    for i in range(turned_ref.shape[1] // CHUNK):
        at = pl.ds(i * CHUNK, CHUNK)
        back = jnp.dot(mixed_ref[...], turned_ref[:, at], preferred_element_type=jnp.float32)
        out_ref[:, at] = (hidden_ref[:, at].astype(jnp.float32) + back).astype(jnp.bfloat16)


def first_kernel(
    hidden_ref, source_ref,
    values_ref, weight0_ref, weight1_ref, turned0_ref, turned1_ref,
    normed_ref, sems,
):
    rows, cols = weight0_ref.shape
    columns = [pl.ds(i * PIECE, PIECE) for i in range(cols // PIECE)]
    copies = []
    for layer, ref in enumerate((weight0_ref, weight1_ref)):
        for at in columns:
            copies.append(
                pltpu.make_async_copy(
                    source_ref.at[pl.ds(layer * rows, rows), at],
                    ref.at[:, at],
                    sems.at[len(copies)],
                )
            )
    for copy in copies:
        copy.start()
    normed_ref[...] = unit(hidden_ref[...])
    for i, at in enumerate(columns):
        copies[i].wait()
        values_ref[:, at] = jnp.dot(
            normed_ref[...], weight0_ref[:, at], preferred_element_type=jnp.float32
        ).astype(jnp.bfloat16)
        turned0_ref[at, :] = weight0_ref[:, at].T
    for i, at in enumerate(columns):
        copies[len(columns) + i].wait()
        turned1_ref[at, :] = weight1_ref[:, at].T


def enter_kernel(hidden_ref, weight_ref, values_ref, normed_ref):
    project(hidden_ref, values_ref, normed_ref, weight_ref)


def keep(stage, active_ref, out_ref, kept_ref):
    @pl.when(active_ref[stage] == 1)
    def _():
        kept_ref[...] = out_ref[...]


def inner_kernel(
    stage,
    active_ref, scale_ref, bias_ref, before_ref, own_ref, after_ref, hidden_ref,
    turned_ref, weight_ref, old_ref,
    out_ref, values_ref, kept_ref,
    mixed_ref, normed_ref,
):
    attend_heads(0, scale_ref, bias_ref, before_ref, own_ref, after_ref, mixed_ref)
    finish(hidden_ref, mixed_ref, out_ref, turned_ref)
    project(out_ref, values_ref, normed_ref, weight_ref)
    keep(stage, active_ref, out_ref, kept_ref)


def leave_kernel(
    stage,
    active_ref, scale_ref, bias_ref, before_ref, own_ref, after_ref, hidden_ref,
    turned_ref, old_ref,
    out_ref, kept_ref,
    mixed_ref,
):
    attend_heads(1, scale_ref, bias_ref, before_ref, own_ref, after_ref, mixed_ref)
    finish(hidden_ref, mixed_ref, out_ref, turned_ref)
    keep(stage, active_ref, out_ref, kept_ref)


VM = pl.BlockSpec(memory_space=pltpu.VMEM)
SM = pl.BlockSpec(memory_space=pltpu.SMEM)
HBM = pl.BlockSpec(memory_space=pltpu.HBM)
CHUNK = 512
PIECE = 256
GROUP = 4


def kernels(tok, width, feat):
    bf = jnp.bfloat16
    weight = pltpu.VMEM((width, feat), bf)
    turned = pltpu.VMEM((feat, width), bf)
    mixed = pltpu.VMEM((tok, feat), bf)
    normed = pltpu.VMEM((tok, width), bf)
    hidden = jax.ShapeDtypeStruct((tok, width), bf)
    values = jax.ShapeDtypeStruct((tok, feat), bf)
    product = 2 * tok * width * feat
    size = 2 * width * feat

    def call(body, ins, outs, scratch, flops, moved, aliases=()):
        return pl.pallas_call(
            body,
            out_shape=outs,
            in_specs=ins,
            out_specs=(VM,) * len(outs),
            scratch_shapes=scratch,
            input_output_aliases=dict(aliases),
            compiler_params=pltpu.CompilerParams(vmem_limit_bytes=6 << 20),
            cost_estimate=pl.CostEstimate(
                flops=int(flops), bytes_accessed=int(moved), transcendentals=0
            ),
        )

    first = call(
        first_kernel, [VM, HBM], (values, weight, weight, turned, turned),
        [normed, pltpu.SemaphoreType.DMA((2 * feat // PIECE,))], product, 4 * size,
    )
    enter = call(enter_kernel, [VM, VM], (values,), [normed], product, size)

    def inner(stage, *args):
        return call(
            functools.partial(inner_kernel, stage), [SM, SM] + [VM] * 8, (hidden, values, hidden),
            [mixed, normed], 2 * product, 2 * size, {9: 2},
        )(*args)

    def leave(stage, *args):
        return call(
            functools.partial(leave_kernel, stage), [SM, SM] + [VM] * 7, (hidden, hidden),
            [mixed], product, size, {8: 1},
        )(*args)

    return first, enter, inner, leave


def on_device(latents, proj, temper, blocks):
    planes = lax.axis_size("x")
    plane = lax.axis_index("x")
    core = lax.axis_index("c")
    dp_count = lax.axis_size("dp")
    dp_index = lax.axis_index("dp")
    micro_count, tok, width = latents.shape
    heads = temper.shape[1]
    feat = proj.shape[2]
    per_dev = tok // BLOCK
    window = 3 * per_dev
    total_blocks = tok * dp_count // BLOCK
    seq_blocks = min(4096, tok * dp_count) // BLOCK

    weights = lax.all_gather(proj[0], ("c", "dp"), axis=0, tiled=True)
    swap = [(0, 1), (1, 0)]
    mine = temper[0]
    other = lax.ppermute(mine, "c", swap)
    both = jnp.where(core == 0, jnp.stack([mine, other]), jnp.stack([other, mine]))
    scale = both * (math.log2(math.e) / math.sqrt(feat // heads))

    chosen = lax.dynamic_index_in_dim(blocks, core, 0, keepdims=False)
    spots = jnp.arange(window, dtype=jnp.int32)
    absolute = (dp_index - 1) * per_dev + spots
    query = dp_index * per_dev + jnp.arange(per_dev, dtype=jnp.int32)
    usable = (
        (absolute >= 0)
        & (absolute < total_blocks)
        & (absolute[None, :] // seq_blocks == query[:, None] // seq_blocks)
    )
    listed = jnp.sum((chosen[..., None] == spots).astype(jnp.int32), axis=2)
    own = (spots[None, :] == per_dev + jnp.arange(per_dev)[:, None]).astype(jnp.int32)
    count = jnp.where(usable[:, None, :], listed, 0) + own[:, None, :]
    bias = jnp.where(count > 0, jnp.log2(jnp.maximum(count, 1).astype(jnp.float32)), NEG)
    bias = jnp.repeat(jnp.transpose(bias, (1, 0, 2)).reshape(heads * per_dev, window), BLOCK, axis=1)

    first, enter, inner, leave = kernels(tok, width, feat)
    up = [(i, i + 1) for i in range(dp_count - 1)]
    down = [(i + 1, i) for i in range(dp_count - 1)]
    hop = [(i, i + 1) for i in range(planes - 1)]

    def beside(values):
        return lax.ppermute(values, "dp", up), lax.ppermute(values, "dp", down)

    hidden = lax.dynamic_index_in_dim(latents, core, 0, keepdims=False)
    active = (plane == jnp.arange(planes)).astype(jnp.int32)
    hidden, scale, bias, active, weights = lax.optimization_barrier(
        (hidden, scale, bias, active, weights)
    )
    kept0 = kept1 = hidden
    for stage in range(planes):
        if stage == 0:
            values, weight0, weight1, turned0, turned1 = first(hidden, weights)
        else:
            (values,) = enter(hidden, weight0)
        before, after = beside(values)
        middle, values, kept0 = inner(
            stage, active, scale, bias, before, values, after, hidden, turned0, weight1, kept0
        )
        before, after = beside(values)
        final, kept1 = leave(
            stage, active, scale, bias, before, values, after, middle, turned1, kept1
        )
        if stage < planes - 1:
            hidden = lax.ppermute(final, "x", hop)
    kept0, kept1, core = lax.optimization_barrier((kept0, kept1, core))
    got = lax.ppermute(jnp.where(core == 0, kept1, kept0), "c", swap)
    states = jnp.where(core == 0, jnp.stack([kept0, got]), jnp.stack([got, kept1]))
    return states[None]


def solution(mesh):
    planes = mesh.devices.shape[0] // 2
    split = Mesh(mesh.devices.reshape(planes, 2, -1), ("x", "c", "dp"))
    placed = (
        P(None, "dp", None),
        P(("x", "c"), "dp", None),
        P(("x", "c"), None),
        P(None, "dp", None, None),
    )
    return jax.shard_map(
        on_device,
        mesh=split,
        in_specs=placed,
        out_specs=P(("x", "c"), None, "dp", None),
        check_vma=False,
    )
```

```python
import functools
import math

import jax
import jax.numpy as jnp
from jax import lax
from jax.experimental import pallas as pl
from jax.experimental.pallas import tpu as pltpu
from jax.sharding import Mesh, PartitionSpec as P

BLOCK = 64
EPS = 1e-06
NEG = -1e30
NT = (((1,), (1,)), ((), ()))


def unit(values):
    wide = values.astype(jnp.float32)
    mean = jnp.mean(wide * wide, axis=-1, keepdims=True)
    return (wide * lax.rsqrt(mean + EPS)).astype(jnp.bfloat16)


def attend_heads(layer, scale_ref, bias_ref, before_ref, own_ref, after_ref, mixed_ref):
    tok, feat = own_ref.shape
    size = 128
    half = tok // 2
    row = lax.broadcasted_iota(jnp.int32, (tok, tok), 0)
    col = lax.broadcasted_iota(jnp.int32, (tok, tok), 1)
    diag = row == col

    def window_of(h):
        at = pl.ds(h * size, size)
        return [ref[:, at] for ref in (before_ref, own_ref, after_ref)]

    def logits_of(h, keys):
        factor = scale_ref[layer, h]
        scores = lax.dot_general(
            keys[1], jnp.concatenate(keys, axis=0), NT, preferred_element_type=jnp.float32
        )
        logits = []
        for i in range(3):
            part = scores[:, i * tok : (i + 1) * tok]
            upper = bias_ref[2 * h : 2 * h + 1, i * tok : (i + 1) * tok]
            lower = bias_ref[2 * h + 1 : 2 * h + 2, i * tok : (i + 1) * tok]
            part = jnp.concatenate(
                [part[:half] * factor + upper, part[half:] * factor + lower], axis=0
            )
            logits.append(jnp.where(diag, NEG, part) if i == 1 else part)
        return logits

    def probs_of(logits):
        top = jnp.max(
            jnp.maximum(jnp.maximum(logits[0], logits[1]), logits[2]), axis=-1, keepdims=True
        )
        return [jnp.exp2(part - top) for part in logits]

    for first in range(0, feat // size, GROUP):
        heads = range(first, first + GROUP)
        windows = [window_of(h) for h in heads]
        keys = [[unit(part) for part in window] for window in windows]
        logits = [logits_of(h, k) for h, k in zip(heads, keys)]
        probs = [probs_of(part) for part in logits]
        for h, window, prob in zip(heads, windows, probs):
            acc = jnp.dot(
                jnp.concatenate([p.astype(jnp.bfloat16) for p in prob], axis=1),
                jnp.concatenate(window, axis=0),
                preferred_element_type=jnp.float32,
            )
            total = jnp.sum(prob[0] + prob[1] + prob[2], axis=-1, keepdims=True)
            mixed_ref[:, pl.ds(h * size, size)] = (acc / total).astype(jnp.bfloat16)


def project(hidden_ref, values_ref, normed_ref, weight_ref):
    normed_ref[...] = unit(hidden_ref[...])
    for i in range(weight_ref.shape[1] // CHUNK):
        at = pl.ds(i * CHUNK, CHUNK)
        values_ref[:, at] = jnp.dot(
            normed_ref[...], weight_ref[:, at], preferred_element_type=jnp.float32
        ).astype(jnp.bfloat16)


def finish(hidden_ref, mixed_ref, out_ref, turned_ref):
    for i in range(turned_ref.shape[1] // CHUNK):
        at = pl.ds(i * CHUNK, CHUNK)
        back = jnp.dot(mixed_ref[...], turned_ref[:, at], preferred_element_type=jnp.float32)
        out_ref[:, at] = (hidden_ref[:, at].astype(jnp.float32) + back).astype(jnp.bfloat16)


def column_copies(source_ref, target_ref, sems, layer):
    rows, cols = target_ref.shape
    copies = []
    for i in range(cols // PIECE):
        at = pl.ds(i * PIECE, PIECE)
        copies.append(
            pltpu.make_async_copy(
                source_ref.at[pl.ds(layer * rows, rows), at], target_ref.at[:, at], sems.at[i]
            )
        )
    return copies


def first_kernel(hidden_ref, source_ref, values_ref, weight_ref, normed_ref, sems):
    copies = column_copies(source_ref, weight_ref, sems, 0)
    for copy in copies:
        copy.start()
    normed_ref[...] = unit(hidden_ref[...])
    for i, copy in enumerate(copies):
        copy.wait()
        at = pl.ds(i * PIECE, PIECE)
        values_ref[:, at] = jnp.dot(
            normed_ref[...], weight_ref[:, at], preferred_element_type=jnp.float32
        ).astype(jnp.bfloat16)


def ready_kernel(weight0_ref, source_ref, weight1_ref, turned0_ref, turned1_ref, sems):
    copies = column_copies(source_ref, weight1_ref, sems, 1)
    for copy in copies:
        copy.start()
    for i in range(len(copies)):
        at = pl.ds(i * PIECE, PIECE)
        turned0_ref[at, :] = weight0_ref[:, at].T
    for i, copy in enumerate(copies):
        copy.wait()
        at = pl.ds(i * PIECE, PIECE)
        turned1_ref[at, :] = weight1_ref[:, at].T


def enter_kernel(stage, active_ref, hidden_ref, weight_ref, values_ref, normed_ref):
    @pl.when(active_ref[stage] == 1)
    def _():
        project(hidden_ref, values_ref, normed_ref, weight_ref)


def inner_kernel(
    stage,
    active_ref, scale_ref, bias_ref, before_ref, own_ref, after_ref, hidden_ref,
    turned_ref, weight_ref, old_ref,
    out_ref, values_ref, kept_ref,
    mixed_ref, normed_ref,
):
    @pl.when(active_ref[stage] == 1)
    def _():
        attend_heads(0, scale_ref, bias_ref, before_ref, own_ref, after_ref, mixed_ref)
        finish(hidden_ref, mixed_ref, out_ref, turned_ref)
        project(out_ref, values_ref, normed_ref, weight_ref)
        kept_ref[...] = out_ref[...]


def leave_kernel(
    stage,
    active_ref, scale_ref, bias_ref, before_ref, own_ref, after_ref, hidden_ref,
    turned_ref, old_ref,
    out_ref, kept_ref,
    mixed_ref,
):
    @pl.when(active_ref[stage] == 1)
    def _():
        attend_heads(1, scale_ref, bias_ref, before_ref, own_ref, after_ref, mixed_ref)
        finish(hidden_ref, mixed_ref, out_ref, turned_ref)
        kept_ref[...] = out_ref[...]


VM = pl.BlockSpec(memory_space=pltpu.VMEM)
SM = pl.BlockSpec(memory_space=pltpu.SMEM)
HBM = pl.BlockSpec(memory_space=pltpu.HBM)
CHUNK = 512
PIECE = 256
GROUP = 4


def kernels(tok, width, feat):
    bf = jnp.bfloat16
    weight = pltpu.VMEM((width, feat), bf)
    turned = pltpu.VMEM((feat, width), bf)
    mixed = pltpu.VMEM((tok, feat), bf)
    normed = pltpu.VMEM((tok, width), bf)
    hidden = jax.ShapeDtypeStruct((tok, width), bf)
    values = jax.ShapeDtypeStruct((tok, feat), bf)
    product = 2 * tok * width * feat
    size = 2 * width * feat

    def call(body, ins, outs, scratch, flops, moved, aliases=(), mib=6):
        return pl.pallas_call(
            body,
            out_shape=outs,
            in_specs=ins,
            out_specs=(VM,) * len(outs),
            scratch_shapes=scratch,
            input_output_aliases=dict(aliases),
            compiler_params=pltpu.CompilerParams(vmem_limit_bytes=mib << 20),
            cost_estimate=pl.CostEstimate(
                flops=int(flops), bytes_accessed=int(moved), transcendentals=0
            ),
        )

    pieces = pltpu.SemaphoreType.DMA((feat // PIECE,))
    first = call(
        first_kernel, [VM, HBM], (values, weight), [normed, pieces], product, 2 * size, (), 44,
    )
    ready = call(
        ready_kernel, [VM, HBM], (weight, turned, turned), [pieces], 2 * product, 4 * size,
    )

    def enter(stage, *args):
        return call(
            functools.partial(enter_kernel, stage), [SM, VM, VM], (values,), [normed], product, size
        )(*args)

    def inner(stage, *args):
        return call(
            functools.partial(inner_kernel, stage), [SM, SM] + [VM] * 8, (hidden, values, hidden),
            [mixed, normed], 2 * product, 2 * size, {9: 2},
        )(*args)

    def leave(stage, *args):
        return call(
            functools.partial(leave_kernel, stage), [SM, SM] + [VM] * 7, (hidden, hidden),
            [mixed], product, size, {8: 1},
        )(*args)

    return first, ready, enter, inner, leave


def on_device(latents, proj, temper, blocks):
    planes = lax.axis_size("x")
    plane = lax.axis_index("x")
    core = lax.axis_index("c")
    dp_count = lax.axis_size("dp")
    dp_index = lax.axis_index("dp")
    micro_count, tok, width = latents.shape
    heads = temper.shape[1]
    feat = proj.shape[2]
    per_dev = tok // BLOCK
    window = 3 * per_dev
    total_blocks = tok * dp_count // BLOCK
    seq_blocks = min(4096, tok * dp_count) // BLOCK

    weights = lax.all_gather(proj[0], ("c", "dp"), axis=0, tiled=True)
    swap = [(0, 1), (1, 0)]
    mine = temper[0]
    other = lax.ppermute(mine, "c", swap)
    both = jnp.where(core == 0, jnp.stack([mine, other]), jnp.stack([other, mine]))
    scale = both * (math.log2(math.e) / math.sqrt(feat // heads))

    chosen = lax.dynamic_index_in_dim(blocks, core, 0, keepdims=False)
    spots = jnp.arange(window, dtype=jnp.int32)
    absolute = (dp_index - 1) * per_dev + spots
    query = dp_index * per_dev + jnp.arange(per_dev, dtype=jnp.int32)
    usable = (
        (absolute >= 0)
        & (absolute < total_blocks)
        & (absolute[None, :] // seq_blocks == query[:, None] // seq_blocks)
    )
    listed = jnp.sum((chosen[..., None] == spots).astype(jnp.int32), axis=2)
    own = (spots[None, :] == per_dev + jnp.arange(per_dev)[:, None]).astype(jnp.int32)
    count = jnp.where(usable[:, None, :], listed, 0) + own[:, None, :]
    bias = jnp.where(count > 0, jnp.log2(jnp.maximum(count, 1).astype(jnp.float32)), NEG)
    bias = jnp.repeat(jnp.transpose(bias, (1, 0, 2)).reshape(heads * per_dev, window), BLOCK, axis=1)

    first, ready, enter, inner, leave = kernels(tok, width, feat)
    up = [(i, i + 1) for i in range(dp_count - 1)]
    down = [(i + 1, i) for i in range(dp_count - 1)]
    hop = [(i, i + 1) for i in range(planes - 1)]

    def beside(values):
        return lax.ppermute(values, "dp", up), lax.ppermute(values, "dp", down)

    hidden = lax.dynamic_index_in_dim(latents, core, 0, keepdims=False)
    active = (plane == jnp.arange(planes)).astype(jnp.int32)
    hidden, scale, bias, active, weights = lax.optimization_barrier(
        (hidden, scale, bias, active, weights)
    )
    kept0 = kept1 = hidden
    for stage in range(planes):
        if stage == 0:
            values, weight0 = first(hidden, weights)
        else:
            (values,) = enter(stage, active, hidden, weight0)
        before, after = beside(values)
        if stage == 0:
            weight1, turned0, turned1 = ready(weight0, weights)
        middle, values, kept0 = inner(
            stage, active, scale, bias, before, values, after, hidden, turned0, weight1, kept0
        )
        before, after = beside(values)
        final, kept1 = leave(
            stage, active, scale, bias, before, values, after, middle, turned1, kept1
        )
        if stage < planes - 1:
            hidden = lax.ppermute(final, "x", hop)
    kept0, kept1, core = lax.optimization_barrier((kept0, kept1, core))
    got = lax.ppermute(jnp.where(core == 0, kept1, kept0), "c", swap)
    states = jnp.where(core == 0, jnp.stack([kept0, got]), jnp.stack([got, kept1]))
    return states[None]


def solution(mesh):
    planes = mesh.devices.shape[0] // 2
    split = Mesh(mesh.devices.reshape(planes, 2, -1), ("x", "c", "dp"))
    placed = (
        P(None, "dp", None),
        P(("x", "c"), "dp", None),
        P(("x", "c"), None),
        P(None, "dp", None, None),
    )
    return jax.shard_map(
        on_device,
        mesh=split,
        in_specs=placed,
        out_specs=P(("x", "c"), None, "dp", None),
        check_vma=False,
    )
```

```python
import functools
import math

import jax
import jax.numpy as jnp
from jax import lax
from jax.experimental import pallas as pl
from jax.experimental.pallas import tpu as pltpu
from jax.sharding import Mesh, PartitionSpec as P

BLOCK = 64
EPS = 1e-06
NEG = -1e30
NT = (((1,), (1,)), ((), ()))


def unit(values):
    wide = values.astype(jnp.float32)
    mean = jnp.mean(wide * wide, axis=-1, keepdims=True)
    return (wide * lax.rsqrt(mean + EPS)).astype(jnp.bfloat16)


def attend_heads(layer, scale_ref, bias_ref, before_ref, own_ref, after_ref, mixed_ref):
    tok, feat = own_ref.shape
    size = 128
    half = tok // 2
    row = lax.broadcasted_iota(jnp.int32, (tok, tok), 0)
    col = lax.broadcasted_iota(jnp.int32, (tok, tok), 1)
    diag = row == col

    def window_of(h):
        at = pl.ds(h * size, size)
        return [ref[:, at] for ref in (before_ref, own_ref, after_ref)]

    def logits_of(h, keys):
        factor = scale_ref[layer, h]
        scores = lax.dot_general(
            keys[1], jnp.concatenate(keys, axis=0), NT, preferred_element_type=jnp.float32
        )
        logits = []
        for i in range(3):
            part = scores[:, i * tok : (i + 1) * tok]
            upper = bias_ref[2 * h : 2 * h + 1, i * tok : (i + 1) * tok]
            lower = bias_ref[2 * h + 1 : 2 * h + 2, i * tok : (i + 1) * tok]
            part = jnp.concatenate(
                [part[:half] * factor + upper, part[half:] * factor + lower], axis=0
            )
            logits.append(jnp.where(diag, NEG, part) if i == 1 else part)
        return logits

    def probs_of(logits):
        top = jnp.max(
            jnp.maximum(jnp.maximum(logits[0], logits[1]), logits[2]), axis=-1, keepdims=True
        )
        return [jnp.exp2(part - top) for part in logits]

    for first in range(0, feat // size, GROUP):
        heads = range(first, first + GROUP)
        windows = [window_of(h) for h in heads]
        keys = [[unit(part) for part in window] for window in windows]
        logits = [logits_of(h, k) for h, k in zip(heads, keys)]
        probs = [probs_of(part) for part in logits]
        for h, window, prob in zip(heads, windows, probs):
            acc = jnp.dot(
                jnp.concatenate([p.astype(jnp.bfloat16) for p in prob], axis=1),
                jnp.concatenate(window, axis=0),
                preferred_element_type=jnp.float32,
            )
            total = jnp.sum(prob[0] + prob[1] + prob[2], axis=-1, keepdims=True)
            mixed_ref[:, pl.ds(h * size, size)] = (acc / total).astype(jnp.bfloat16)


def project(hidden_ref, values_ref, normed_ref, weight_ref):
    normed_ref[...] = unit(hidden_ref[...])
    for i in range(weight_ref.shape[1] // CHUNK):
        at = pl.ds(i * CHUNK, CHUNK)
        values_ref[:, at] = jnp.dot(
            normed_ref[...], weight_ref[:, at], preferred_element_type=jnp.float32
        ).astype(jnp.bfloat16)


def finish(hidden_ref, mixed_ref, out_ref, turned_ref):
    for i in range(turned_ref.shape[1] // CHUNK):
        at = pl.ds(i * CHUNK, CHUNK)
        back = jnp.dot(mixed_ref[...], turned_ref[:, at], preferred_element_type=jnp.float32)
        out_ref[:, at] = (hidden_ref[:, at].astype(jnp.float32) + back).astype(jnp.bfloat16)


def column_copies(source_ref, target_ref, sems, layer):
    rows, cols = target_ref.shape
    copies = []
    for i in range(cols // PIECE):
        at = pl.ds(i * PIECE, PIECE)
        copies.append(
            pltpu.make_async_copy(
                source_ref.at[pl.ds(layer * rows, rows), at], target_ref.at[:, at], sems.at[i]
            )
        )
    return copies


def first_kernel(hidden_ref, source_ref, values_ref, weight_ref, normed_ref, total_ref, sems):
    pieces = weight_ref.shape[0] // CHUNK
    copies = []
    for i in range(pieces):
        at = pl.ds(i * CHUNK, CHUNK)
        copies.append(
            pltpu.make_async_copy(source_ref.at[at, :], weight_ref.at[at, :], sems.at[i])
        )
        copies[-1].start()
    normed_ref[...] = unit(hidden_ref[...])
    for i, copy in enumerate(copies):
        copy.wait()
        at = pl.ds(i * CHUNK, CHUNK)
        part = jnp.dot(
            normed_ref[:, at], weight_ref[at, :], preferred_element_type=jnp.float32
        )
        if i == 0:
            total_ref[...] = part
        elif i < pieces - 1:
            total_ref[...] += part
        else:
            values_ref[...] = (total_ref[...] + part).astype(jnp.bfloat16)


def ready_kernel(weight0_ref, source_ref, weight1_ref, turned0_ref, turned1_ref, sems):
    copies = column_copies(source_ref, weight1_ref, sems, 1)
    for copy in copies:
        copy.start()
    for i in range(len(copies)):
        at = pl.ds(i * PIECE, PIECE)
        turned0_ref[at, :] = weight0_ref[:, at].T
    for i, copy in enumerate(copies):
        copy.wait()
        at = pl.ds(i * PIECE, PIECE)
        turned1_ref[at, :] = weight1_ref[:, at].T


def enter_kernel(stage, active_ref, hidden_ref, weight_ref, values_ref, normed_ref):
    @pl.when(active_ref[stage] == 1)
    def _():
        project(hidden_ref, values_ref, normed_ref, weight_ref)


def inner_kernel(
    stage,
    active_ref, scale_ref, bias_ref, before_ref, own_ref, after_ref, hidden_ref,
    turned_ref, weight_ref, old_ref,
    out_ref, values_ref, kept_ref,
    mixed_ref, normed_ref,
):
    @pl.when(active_ref[stage] == 1)
    def _():
        attend_heads(0, scale_ref, bias_ref, before_ref, own_ref, after_ref, mixed_ref)
        finish(hidden_ref, mixed_ref, out_ref, turned_ref)
        project(out_ref, values_ref, normed_ref, weight_ref)
        kept_ref[...] = out_ref[...]


def leave_kernel(
    stage,
    active_ref, scale_ref, bias_ref, before_ref, own_ref, after_ref, hidden_ref,
    turned_ref, old_ref,
    out_ref, kept_ref,
    mixed_ref,
):
    @pl.when(active_ref[stage] == 1)
    def _():
        attend_heads(1, scale_ref, bias_ref, before_ref, own_ref, after_ref, mixed_ref)
        finish(hidden_ref, mixed_ref, out_ref, turned_ref)
        kept_ref[...] = out_ref[...]


VM = pl.BlockSpec(memory_space=pltpu.VMEM)
SM = pl.BlockSpec(memory_space=pltpu.SMEM)
HBM = pl.BlockSpec(memory_space=pltpu.HBM)
CHUNK = 512
PIECE = 256
GROUP = 4


def kernels(tok, width, feat):
    bf = jnp.bfloat16
    weight = pltpu.VMEM((width, feat), bf)
    turned = pltpu.VMEM((feat, width), bf)
    mixed = pltpu.VMEM((tok, feat), bf)
    normed = pltpu.VMEM((tok, width), bf)
    hidden = jax.ShapeDtypeStruct((tok, width), bf)
    values = jax.ShapeDtypeStruct((tok, feat), bf)
    product = 2 * tok * width * feat
    size = 2 * width * feat

    def call(body, ins, outs, scratch, flops, moved, aliases=(), mib=6):
        return pl.pallas_call(
            body,
            out_shape=outs,
            in_specs=ins,
            out_specs=(VM,) * len(outs),
            scratch_shapes=scratch,
            input_output_aliases=dict(aliases),
            compiler_params=pltpu.CompilerParams(vmem_limit_bytes=mib << 20),
            cost_estimate=pl.CostEstimate(
                flops=int(flops), bytes_accessed=int(moved), transcendentals=0
            ),
        )

    pieces = pltpu.SemaphoreType.DMA((feat // PIECE,))
    by_rows = pltpu.SemaphoreType.DMA((width // CHUNK,))
    first = call(
        first_kernel, [VM, HBM], (values, weight), [normed, pltpu.VMEM((tok, feat), jnp.float32), by_rows], product, 2 * size, (), 44,
    )
    ready = call(
        ready_kernel, [VM, HBM], (weight, turned, turned), [pieces], 2 * product, 4 * size,
    )

    def enter(stage, *args):
        return call(
            functools.partial(enter_kernel, stage), [SM, VM, VM], (values,), [normed], product, size
        )(*args)

    def inner(stage, *args):
        return call(
            functools.partial(inner_kernel, stage), [SM, SM] + [VM] * 8, (hidden, values, hidden),
            [mixed, normed], 2 * product, 2 * size, {9: 2},
        )(*args)

    def leave(stage, *args):
        return call(
            functools.partial(leave_kernel, stage), [SM, SM] + [VM] * 7, (hidden, hidden),
            [mixed], product, size, {8: 1},
        )(*args)

    return first, ready, enter, inner, leave


def on_device(latents, proj, temper, blocks):
    planes = lax.axis_size("x")
    plane = lax.axis_index("x")
    core = lax.axis_index("c")
    dp_count = lax.axis_size("dp")
    dp_index = lax.axis_index("dp")
    micro_count, tok, width = latents.shape
    heads = temper.shape[1]
    feat = proj.shape[2]
    per_dev = tok // BLOCK
    window = 3 * per_dev
    total_blocks = tok * dp_count // BLOCK
    seq_blocks = min(4096, tok * dp_count) // BLOCK

    weights = lax.all_gather(proj[0], ("c", "dp"), axis=0, tiled=True)
    swap = [(0, 1), (1, 0)]
    mine = temper[0]
    other = lax.ppermute(mine, "c", swap)
    both = jnp.where(core == 0, jnp.stack([mine, other]), jnp.stack([other, mine]))
    scale = both * (math.log2(math.e) / math.sqrt(feat // heads))

    chosen = lax.dynamic_index_in_dim(blocks, core, 0, keepdims=False)
    spots = jnp.arange(window, dtype=jnp.int32)
    absolute = (dp_index - 1) * per_dev + spots
    query = dp_index * per_dev + jnp.arange(per_dev, dtype=jnp.int32)
    usable = (
        (absolute >= 0)
        & (absolute < total_blocks)
        & (absolute[None, :] // seq_blocks == query[:, None] // seq_blocks)
    )
    listed = jnp.sum((chosen[..., None] == spots).astype(jnp.int32), axis=2)
    own = (spots[None, :] == per_dev + jnp.arange(per_dev)[:, None]).astype(jnp.int32)
    count = jnp.where(usable[:, None, :], listed, 0) + own[:, None, :]
    bias = jnp.where(count > 0, jnp.log2(jnp.maximum(count, 1).astype(jnp.float32)), NEG)
    bias = jnp.repeat(jnp.transpose(bias, (1, 0, 2)).reshape(heads * per_dev, window), BLOCK, axis=1)

    first, ready, enter, inner, leave = kernels(tok, width, feat)
    up = [(i, i + 1) for i in range(dp_count - 1)]
    down = [(i + 1, i) for i in range(dp_count - 1)]
    hop = [(i, i + 1) for i in range(planes - 1)]

    def beside(values):
        return lax.ppermute(values, "dp", up), lax.ppermute(values, "dp", down)

    hidden = lax.dynamic_index_in_dim(latents, core, 0, keepdims=False)
    active = (plane == jnp.arange(planes)).astype(jnp.int32)
    hidden, scale, bias, active, weights = lax.optimization_barrier(
        (hidden, scale, bias, active, weights)
    )
    kept0 = kept1 = hidden
    for stage in range(planes):
        if stage == 0:
            values, weight0 = first(hidden, weights)
        else:
            (values,) = enter(stage, active, hidden, weight0)
        before, after = beside(values)
        if stage == 0:
            weight1, turned0, turned1 = ready(weight0, weights)
        middle, values, kept0 = inner(
            stage, active, scale, bias, before, values, after, hidden, turned0, weight1, kept0
        )
        before, after = beside(values)
        final, kept1 = leave(
            stage, active, scale, bias, before, values, after, middle, turned1, kept1
        )
        if stage < planes - 1:
            hidden = lax.ppermute(final, "x", hop)
    kept0, kept1, core = lax.optimization_barrier((kept0, kept1, core))
    got = lax.ppermute(jnp.where(core == 0, kept1, kept0), "c", swap)
    states = jnp.where(core == 0, jnp.stack([kept0, got]), jnp.stack([got, kept1]))
    return states[None]


def solution(mesh):
    planes = mesh.devices.shape[0] // 2
    split = Mesh(mesh.devices.reshape(planes, 2, -1), ("x", "c", "dp"))
    placed = (
        P(None, "dp", None),
        P(("x", "c"), "dp", None),
        P(("x", "c"), None),
        P(None, "dp", None, None),
    )
    return jax.shard_map(
        on_device,
        mesh=split,
        in_specs=placed,
        out_specs=P(("x", "c"), None, "dp", None),
        check_vma=False,
    )
```
